32 devices in a mesh: dp: 8 (over z, x), section: 4 (over y, core).
Axes of the slice: x: 2, y: 2, z: 4, core: 2. Of those that a mesh axis runs over, the one named last changes fastest.
Arguments:
- saved_inputs: bfloat16 [4, 6144, 1024], P('section', 'dp'), may hold values from -6 to 6
- cotangent: bfloat16 [6144, 1024], P('dp'), may hold values from -6 to 6
- pack_lists: int32 [8, 768], P('dp'), may hold values from 0 to 767, each once within a row
- segment_ids: int32 [96, 64], P('dp'), may hold values from 0 to 7, never falling along the last dimension, each value on 1 to 32 neighbouring positions
- w_in: bfloat16 [4, 1024, 4096], P('section'), may hold values from -0.1875 to 0.1875
- w_out: bfloat16 [4, 1024, 1024], P('section'), may hold values from -0.1875 to 0.1875
Outputs:
- grad_inputs: bfloat16 [4, 6144, 1024], P('section', 'dp')
- grad_w_in: float32 [4, 1024, 4096], P('section', 'dp')
- grad_w_out: float32 [4, 1024, 1024], P('section', 'dp')
The draws below stay inside these ranges and needn't reach their ends.
Inputs may be any that keep to these rules, and one draw needn't show every extreme that they name: `pack_lists`: each row is an ordering of the rows of one loader rank; its k-th block of equal length names the rows sent to packed rank k. `segment_ids`: ids never fall along a micro-batch; a history is the run of one id, 1 to 32 rows, and one has exactly 32.
All inputs are finite; a program needn't handle non-finite values.
Results may differ from the reference program's by a relative error of at most 0.03.
Values may be sent and summed in bfloat16 or wider, within the bound.
A program may use at most 128 MiB of HBM per device.

```python
import math
import jax
import jax.numpy as jnp
import numpy as np
from jax import lax

D = 1024
H = 16
MB_ROWS = 64
SEQ_MAX = 8
TOK_DEV = 768
TOKENS = 6144
LAYERS = 4
N_DP = 8
N_SECTION = 4


def raised(entries, rng, source, target, blocks, factor):
    def block_of(dim):
        return (jnp.arange(entries.shape[dim]) // (entries.shape[dim] // blocks)).reshape((-1,) + (1,) * (entries.ndim - 1 - dim))

    one_side = jax.random.permutation(rng, blocks)[block_of(target)]
    second = (block_of(target) + blocks // 2) % blocks
    return jnp.where((block_of(source) == one_side) | (block_of(source) == second), factor * entries, entries)


def levels(rng, dims, shards, smallest, high):
    factor_of = 1.0
    for axis_at, parts in shards:
        steps = jax.random.uniform(jax.random.fold_in(jax.random.fold_in(rng, 6), axis_at), (parts,), jnp.float32, smallest / len(shards), high / len(shards))
        factor_of = factor_of * jnp.repeat(jnp.exp(steps), dims[axis_at] // parts).reshape((-1,) + (1,) * (len(dims) - 1 - axis_at))
    return factor_of


def split_up(number_of, total, most, skew):
    weights = [(1 << 20) // math.isqrt(grade ** skew) + 1 for grade in range(2, number_of + 1)]
    spare, holding = total - most - (number_of - 1), [1] * (number_of - 1)
    while spare > 0:
        free = [i for i in range(number_of - 1) if holding[i] < most]
        pool, left = sum([weights[i] for i in free]), spare
        for i in free:
            extra = min(most - holding[i], max(1, left * weights[i] // pool), spare)
            holding[i] = holding[i] + extra
            spare = spare - extra
    return np.array([most] + holding)


def uneven_parts(stream_key, amount, total, bound, skew):
    if amount == 2:
        one = jax.random.randint(stream_key, (), max(1, total - bound), min(bound, total - 1) + 1)
        return jnp.stack([one, total - one])
    lengths = jnp.asarray(split_up(amount, total, bound, skew), jnp.int32)
    couples = (amount - 1) // 2
    donor, receiver = lengths[1:1 + 2 * couples:2], lengths[2:2 + 2 * couples:2]
    room = jnp.minimum(donor - 1, bound - receiver)
    moved = jax.random.randint(jax.random.fold_in(stream_key, 1), (couples,), 0, 1 << 20) % (room + 1)
    lengths = lengths.at[1:1 + 2 * couples:2].set(donor - moved).at[2:2 + 2 * couples:2].set(receiver + moved)
    return lengths[jax.random.permutation(jax.random.fold_in(stream_key, 2), amount)]


def normal_values(own_key, shape, spread, reach, shards=(), dtype=jnp.bfloat16):
    drawn = spread * jax.random.normal(own_key, shape, jnp.float32)
    if shards:
        drawn = drawn * levels(own_key, shape, shards, -0.22, 0.18)
    return jnp.clip(drawn, -reach, reach).astype(dtype)


def heavy_noise(rng, shape, deviation, bound, shards, heavy, kind=jnp.bfloat16):
    array = deviation * jax.random.normal(rng, shape, jnp.float32)
    if shards:
        array = array * levels(rng, shape, shards, -0.22, 0.18)
    return jnp.clip(raised(array, jax.random.fold_in(rng, 3), *heavy), -bound, bound).astype(kind)


def setup_inputs(seed: int = 0) -> dict:
    splits = jax.random.split(jax.random.key(seed), 7)
    return {
        "saved_inputs": heavy_noise(splits[0], (LAYERS, TOKENS, D), 1.0, 6.0, ((0, 4), (1, 8)), (1, 2, 8, 2.0)),
        "cotangent": normal_values(splits[1], (TOKENS, D), 1.0, 6.0, ((0, 8),)),
        "pack_lists": jax.vmap(lambda own: jax.random.permutation(own, TOK_DEV))(jax.random.split(splits[2], N_DP)).reshape((N_DP, TOK_DEV)).astype(jnp.int32),
        "segment_ids": jax.vmap(lambda own: jnp.searchsorted(jnp.cumsum(uneven_parts(own, SEQ_MAX, MB_ROWS, MB_ROWS // 2, 2)), jnp.arange(MB_ROWS), side="right"))(jax.random.split(splits[3], (TOKENS // MB_ROWS))).reshape((TOKENS // MB_ROWS, MB_ROWS)).astype(jnp.int32),
        "w_in": normal_values(splits[4], (LAYERS, D, 4 * D), D ** -0.5, 0.1875, ((0, 4),)),
        "w_out": normal_values(splits[5], (LAYERS, D, D), D ** -0.5, 0.1875, ((0, 4),)),
    }


def norm_rows(values):
    centered = values - lax.optimization_barrier(jnp.mean(values, axis=-1, keepdims=True))
    variance = lax.optimization_barrier(jnp.mean(centered * centered, axis=-1, keepdims=True))
    return centered * lax.rsqrt(variance + 1e-05)

def mixer(pre, segments):
    row_count = pre.shape[0]
    model_width = pre.shape[1] // 4
    head_dim = model_width // H
    active = jax.nn.silu(pre)
    gate_part = active[:, :model_width]
    value_part = active[:, model_width:2 * model_width].astype(jnp.bfloat16).reshape(row_count, H, head_dim)
    query_part = active[:, 2 * model_width:3 * model_width].astype(jnp.bfloat16).reshape(row_count, H, head_dim)
    key_part = active[:, 3 * model_width:].astype(jnp.bfloat16).reshape(row_count, H, head_dim)
    scores = jnp.einsum('ihd,jhd->hij', query_part, key_part, preferred_element_type=jnp.float32) / jnp.sqrt(jnp.float32(head_dim))
    positions = jnp.arange(row_count)
    allowed = (segments[:, None] == segments[None, :]) & (positions[None, :] <= positions[:, None])
    weights = (jax.nn.silu(scores) * allowed.astype(jnp.float32) / row_count).astype(jnp.bfloat16)
    mixed = jnp.einsum('hij,jhd->ihd', weights, value_part, preferred_element_type=jnp.float32).reshape(row_count, model_width)
    return norm_rows(mixed) * gate_part

def times_transpose(left, right):
    return lax.dot_general(left, right, (((1,), (1,)), ((), ())), preferred_element_type=jnp.float32)

def layer_grads(inputs_here, grad_here, segments, weight_in, weight_out):
    normed, norm_back = jax.vjp(norm_rows, inputs_here.astype(jnp.float32))
    normed_b = normed.astype(jnp.bfloat16)
    pre = jnp.dot(normed_b, weight_in, preferred_element_type=jnp.float32)
    mixed, mix_back = jax.vjp(lambda value_in: mixer(value_in, segments), pre)
    mixed_b = mixed.astype(jnp.bfloat16)
    grad_mixed = times_transpose(grad_here, weight_out).astype(jnp.bfloat16)
    grad_pre = mix_back(grad_mixed.astype(jnp.float32))[0].astype(jnp.bfloat16)
    grad_normed = times_transpose(grad_pre, weight_in)
    grad_x = (grad_here.astype(jnp.float32) + norm_back(grad_normed)[0]).astype(jnp.bfloat16)
    return (grad_x, normed_b, grad_pre, mixed_b)

def contract_rows(left, right):
    return lax.dot_general(left, right, (((0,), (0,)), ((), ())), preferred_element_type=jnp.float32)

def reference(saved_inputs, cotangent, pack_lists, segment_ids, w_in, w_out):
    share = TOK_DEV // N_DP
    loader = cotangent.reshape(N_DP, TOK_DEV, D)
    picked = loader[jnp.arange(N_DP)[:, None], pack_lists]
    packed = picked.reshape(N_DP, N_DP, share, D).transpose(1, 0, 2, 3).reshape(TOKENS, D)
    batches = TOKENS // MB_ROWS
    grad_here = packed.reshape(batches, MB_ROWS, D)
    input_grads = []
    in_grads = []
    out_grads = []
    for layer in range(N_SECTION - 1, -1, -1):
        inputs_here = saved_inputs[layer].reshape(batches, MB_ROWS, D)
        grad_x, normed_b, grad_pre, mixed_b = jax.vmap(layer_grads, in_axes=(0, 0, 0, None, None))(inputs_here, grad_here, segment_ids, w_in[layer], w_out[layer])
        in_grads.append(contract_rows(normed_b.reshape(TOKENS, D), grad_pre.reshape(TOKENS, 4 * D)))
        out_grads.append(contract_rows(mixed_b.reshape(TOKENS, D), grad_here.reshape(TOKENS, D)))
        input_grads.append(grad_x.reshape(TOKENS, D))
        grad_here = grad_x
    grad_inputs = jnp.stack(input_grads[::-1])
    grad_w_in = jnp.stack(in_grads[::-1])
    grad_w_out = jnp.stack(out_grads[::-1])
    return (grad_inputs, grad_w_in, grad_w_out)
```

```python
import functools

import jax
import jax.numpy as jnp
from jax import lax
from jax.experimental import pallas as pl
from jax.experimental.pallas import tpu as pltpu
from jax.sharding import PartitionSpec as P

H = 16
F_BATCHES = 3
B_BATCHES = 2
LAG = 1
HOP_LAG = 3
BF = jnp.bfloat16
F32 = jnp.float32
VMEM_LIMIT = 60 * 1024 * 1024


def mm(a, b):
    return lax.dot_general(a, b, (((1,), (0,)), ((), ())), preferred_element_type=F32)


def mm_t(a, b):
    return lax.dot_general(a, b, (((1,), (1,)), ((), ())), preferred_element_type=F32)


def t_mm(a, b):
    return lax.dot_general(a, b, (((0,), (0,)), ((), ())), preferred_element_type=F32)


def sigmoid(x):
    return 0.5 * jnp.tanh(0.5 * x) + 0.5


def stacked(part, mask, copies):
    return jnp.concatenate([part] * copies, axis=0) * mask


def norm_stats(values):
    centered = values - jnp.mean(values, axis=-1, keepdims=True)
    variance = jnp.mean(centered * centered, axis=-1, keepdims=True)
    inv = lax.rsqrt(variance + 1e-05)
    return centered * inv, inv


def forward_kernel(
    rows, dp_count, sections, x_ref, w_ref, mask_ref, bm_ref, picked_ref,
    win_part_ref, wout_part_ref,
    packed_ref, xy_ref, gate_ref, mhat_ref, vqk_ref, slope_ref, att_ref, sfac_ref, rx_ref, rm_ref,
    win_t_ref, wout_t_ref, send_sem, recv_sem, own_sem,
):
    step = pl.program_id(0)
    sender = lax.axis_index("section") == sections - 1
    me = lax.axis_index("dp")
    own = pltpu.make_async_copy(picked_ref.at[me], packed_ref.at[me], own_sem)

    def hop(offset):
        peer = (me + offset) % dp_count
        return pltpu.make_async_remote_copy(
            src_ref=picked_ref.at[peer],
            dst_ref=packed_ref.at[me],
            send_sem=send_sem.at[offset - 1],
            recv_sem=recv_sem.at[offset - 1],
            device_id={"dp": peer},
            device_id_type=pl.DeviceIdType.MESH,
        )

    @pl.when((step == 0) & sender)
    def _():
        barrier = pltpu.get_barrier_semaphore()
        for offset in range(1, dp_count):
            pl.semaphore_signal(
                barrier, inc=1, device_id={"dp": (me + offset) % dp_count},
                device_id_type=pl.DeviceIdType.MESH,
            )
        pl.semaphore_wait(barrier, dp_count - 1)
        own.start()
        for offset in range(1, dp_count):
            hop(offset).start()

    width = x_ref.shape[1]
    group = bm_ref.shape[0]
    copies = group // rows
    head_dim = width // H
    xn, rx = norm_stats(x_ref[...].astype(F32))
    xy_ref[:, :width] = xn.astype(BF)
    rx_ref[...] = jnp.broadcast_to(rx, rx_ref.shape)
    win_t_ref[...] = win_part_ref[...].T
    wout_t_ref[...] = wout_part_ref[...].T
    for part in range(4):
        cols = slice(part * width, (part + 1) * width)
        pre = mm(xy_ref[:, :width], w_ref[:, cols])
        sig = sigmoid(pre)
        act = pre * sig
        slope_ref[:, cols] = (sig + act * (1.0 - sig)).astype(BF)
        if part == 0:
            gate_ref[...] = act.astype(BF)
        else:
            vqk_ref[:, (part - 1) * width : part * width] = act.astype(BF)
    block_mask = bm_ref[...]
    scale = 1.0 / head_dim ** 0.5
    for micro in range(x_ref.shape[0] // rows):
        r = slice(micro * rows, (micro + 1) * rows)
        allowed = jnp.concatenate([mask_ref[r, :]] * (group // mask_ref.shape[1]), axis=1)
        mixed = []
        for lo in range(0, width, group):
            c = slice(lo, lo + group)
            v = vqk_ref[r, lo : lo + group]
            q = vqk_ref[r, width + lo : width + lo + group]
            k = vqk_ref[r, 2 * width + lo : 2 * width + lo + group]
            scores = mm_t(q, stacked(k, block_mask, copies)) * scale
            sig = sigmoid(scores)
            act = scores * sig
            att = (act * allowed).astype(BF)
            att_ref[r, c] = att
            sfac_ref[r, c] = ((sig + act * (1.0 - sig)) * allowed * scale).astype(BF)
            mixed.append(mm(att, stacked(v, block_mask, copies)))
        mixed = jnp.concatenate(mixed, axis=1)
        mhat, rm = norm_stats(mixed)
        mhat_ref[r, :] = mhat.astype(BF)
        rm_ref[r, :] = jnp.broadcast_to(rm, (rows, rm_ref.shape[1]))
        xy_ref[r, width:] = (mhat * gate_ref[r, :].astype(F32)).astype(BF)

    @pl.when((step == pl.num_programs(0) - 1) & sender)
    def _():
        own.wait()
        for offset in range(1, dp_count):
            back = pltpu.make_async_remote_copy(
                src_ref=picked_ref.at[me],
                dst_ref=packed_ref.at[(me + dp_count - offset) % dp_count],
                send_sem=send_sem.at[offset - 1],
                recv_sem=recv_sem.at[offset - 1],
                device_id={"dp": (me + offset) % dp_count},
                device_id_type=pl.DeviceIdType.MESH,
            )
            back.wait_recv()
            hop(offset).wait_send()


def backward_kernel(
    rows, sections, g0_ref, win_ref, wout_ref, bm_ref, xn_ref, gate_ref, mhat_ref, vqk_ref,
    slope_ref, att_ref, sfac_ref, rx_ref, rm_ref,
    dx_ref, dpre_ref, arrived, leaving, send_sem, recv_sem,
):
    step = pl.program_id(0)
    steps = pl.num_programs(0)
    section = lax.axis_index("section")
    last = sections - 1
    width = g0_ref.shape[1]
    wide = 4 * width
    group = bm_ref.shape[0]
    copies = group // rows
    before = jnp.maximum(section - 1, 0)
    after = jnp.minimum(section + 1, last)

    def hop(slot):
        return pltpu.make_async_remote_copy(
            src_ref=leaving.at[slot],
            dst_ref=arrived.at[slot],
            send_sem=send_sem.at[slot],
            recv_sem=recv_sem.at[slot],
            device_id={"section": before},
            device_id_type=pl.DeviceIdType.MESH,
        )

    @pl.when(step == 0)
    def _():
        barrier = pltpu.get_barrier_semaphore()

        @pl.when(section > 0)
        def _():
            pl.semaphore_signal(
                barrier, inc=1, device_id={"section": before}, device_id_type=pl.DeviceIdType.MESH
            )

        @pl.when(section < last)
        def _():
            pl.semaphore_signal(
                barrier, inc=1, device_id={"section": after}, device_id_type=pl.DeviceIdType.MESH
            )

        peers = (section > 0).astype(jnp.int32) + (section < last).astype(jnp.int32)
        pl.semaphore_wait(barrier, peers)

    @pl.when(section == last)
    def _():
        dpre_ref[:, wide:] = g0_ref[...]

    @pl.when(section < last)
    def _():
        hop(step).wait_recv()
        dpre_ref[:, wide:] = arrived[step]

    gyu = mm(dpre_ref[:, wide:], wout_ref[...]).astype(BF).astype(F32)
    dpre_ref[:, :width] = (gyu * mhat_ref[...].astype(F32) * slope_ref[:, :width].astype(F32)).astype(BF)
    block_mask = bm_ref[...]
    block_mask_f = block_mask.astype(F32)

    def fold(full):
        full = full * block_mask_f
        total = full[:rows]
        for copy in range(1, copies):
            total = total + full[copy * rows : (copy + 1) * rows]
        return total.astype(BF).astype(F32)

    for micro in range(g0_ref.shape[0] // rows):
        r = slice(micro * rows, (micro + 1) * rows)
        dn = gyu[r, :] * gate_ref[r, :].astype(F32)
        mhat = mhat_ref[r, :].astype(F32)
        mean_d = jnp.mean(dn, axis=-1, keepdims=True)
        mean_p = jnp.mean(dn * mhat, axis=-1, keepdims=True)
        dm = (rm_ref[r, :1] * (dn - mean_d - mhat * mean_p)).astype(BF)
        for lo in range(0, width, group):
            c = slice(lo, lo + group)
            cv = slice(lo, lo + group)
            cq = slice(width + lo, width + lo + group)
            ck = slice(2 * width + lo, 2 * width + lo + group)
            dmg = dm[:, lo : lo + group]
            datt = mm_t(dmg, stacked(vqk_ref[r, cv], block_mask, copies)).astype(BF).astype(F32)
            ds = (datt * sfac_ref[r, c].astype(F32)).astype(BF)
            dv = fold(t_mm(att_ref[r, c], dmg))
            dq = mm(ds, stacked(vqk_ref[r, ck], block_mask, copies)).astype(BF).astype(F32)
            dk = fold(t_mm(ds, vqk_ref[r, cq]))
            for part, value in ((1, dv), (2, dq), (3, dk)):
                cols = slice(part * width + lo, part * width + lo + group)
                dpre_ref[r, cols] = (value * slope_ref[r, cols].astype(F32)).astype(BF)
    dn = mm(dpre_ref[:, :wide], win_ref[...])
    xn = xn_ref[...].astype(F32)
    mean_d = jnp.mean(dn, axis=-1, keepdims=True)
    mean_p = jnp.mean(dn * xn, axis=-1, keepdims=True)
    dx = (dpre_ref[:, wide:].astype(F32) + rx_ref[:, :1] * (dn - mean_d - xn * mean_p)).astype(BF)
    dx_ref[...] = dx

    @pl.when(section > 0)
    def _():
        leaving[step] = dx
        hop(step).start()

    @pl.when((section > 0) & (step == steps - 1))
    def _():
        def finish(slot, carry):
            hop(slot).wait_send()
            return carry

        lax.fori_loop(0, steps, finish, 0)


class Line:
    def __init__(self, count, me, device, at, own, landed, send_sem, recv_sem):
        self.count, self.me, self.device, self.at = count, me, device, at
        self.own, self.landed = own, landed
        self.send_sem, self.recv_sem = send_sem, recv_sem

    def base(self, me):
        return self.count - me if me > 0 else 0

    def copy(self, src, slot, shard, peer):
        return pltpu.make_async_remote_copy(
            src_ref=src,
            dst_ref=self.landed.at[self.at, slot],
            send_sem=self.send_sem.at[self.at, shard],
            recv_sem=self.recv_sem.at[self.at, slot],
            device_id=self.device(peer),
            device_id_type=pl.DeviceIdType.MESH,
        )

    def arrive(self, slot):
        self.copy(self.landed.at[self.at, slot], slot, 0, 0).wait_recv()

    def start(self):
        last = self.count - 1

        @pl.when(self.me == 0)
        def _():
            for shard in range(last, 0, -1):
                self.copy(self.own(shard), shard - 1, shard, 1).start()

        @pl.when(self.me == last)
        def _():
            for shard in range(last):
                self.copy(self.own(shard), self.base(last - 1) + shard, shard, last - 1).start()

    def pass_on(self, slot, shard, to_slot, peer):
        self.arrive(slot)
        ref = self.landed.at[self.at, slot]
        ref[...] = (ref[...].astype(F32) + self.own(shard)[...].astype(F32)).astype(BF)
        self.copy(ref, to_slot, shard, peer).start()

    def stage(self, number):
        up, down = number, self.count - 1 - number

        @pl.when(self.me == up)
        def _():
            for shard in range(self.count - 1, up, -1):
                self.pass_on(shard - up, shard, shard - up - 1, up + 1)
            self.arrive(0)

        @pl.when(self.me == down)
        def _():
            for shard in range(down):
                self.pass_on(self.base(down) + shard, shard, self.base(down - 1) + shard, down - 1)
            self.arrive(self.base(down) + down)

    def finish(self, out):
        inner = (self.me > 0) & (self.me < self.count - 1)
        total = self.own(self.me)[...].astype(F32) + self.landed[self.at, 0].astype(F32)
        if self.count == 2:
            out(total)
        else:
            @pl.when(inner)
            def _():
                out(total + self.landed[self.at, self.count].astype(F32))

            @pl.when(jnp.logical_not(inner))
            def _():
                out(total)

    def sent(self):
        for offset in range(1, self.count):
            shard = (self.me + offset) % self.count
            self.copy(self.own(shard), 0, shard, 0).wait_send()


def weight_kernel(
    nx, nz, tiles, in_tiles, z_tiles, left_ref, right_ref, win_ref, wout_ref,
    x_own, x_first, x_second, z_own, z_first, z_second,
    xs1, xr1, xs2, xr2, zs1, zr1, zs2, zr2,
):
    step = pl.program_id(0)
    me = lax.axis_index("dp")
    my_z = me // nx
    my_x = me % nx
    rows = win_ref.shape[0]
    period = tiles // z_tiles
    last_lag = LAG + HOP_LAG * (nx + nz - 2)

    def device(z, x):
        return {"dp": z * nx + x}

    def on_x(peer):
        return device(my_z, peer)

    def on_z(peer):
        return device(peer, my_x)

    def is_z(tile):
        return (tile % period == 0) & (tile // period < z_tiles)

    def lines(kind, tile):
        if kind == "z":
            at = tile // period
            first = Line(nz, my_z, on_z, at, lambda j: z_own.at[at, j], z_first, zs1, zr1)
            second = Line(
                nx, my_x, on_x, at, lambda j: z_own.at[at, my_z, pl.ds(j * rows, rows)], z_second, zs2, zr2
            )
        else:
            at = tile - jnp.minimum((tile + period - 1) // period, z_tiles)
            first = Line(nx, my_x, on_x, at, lambda j: x_own.at[at, j], x_first, xs1, xr1)
            second = Line(
                nz, my_z, on_z, at, lambda j: x_own.at[at, my_x, pl.ds(j * rows, rows)], x_second, xs2, xr2
            )
        return first, second

    @pl.when(step == 0)
    def _():
        barrier = pltpu.get_barrier_semaphore()
        greeted = 0
        for mine, count, to in ((my_x, nx, on_x), (my_z, nz, on_z)):
            for has, peer in ((mine > 0, mine - 1), (mine < count - 1, mine + 1)):
                @pl.when(has)
                def _(peer=peer, to=to):
                    pl.semaphore_signal(
                        barrier, inc=1, device_id=to(peer), device_id_type=pl.DeviceIdType.MESH
                    )

                greeted = greeted + has.astype(jnp.int32)
        pl.semaphore_wait(barrier, greeted)

    @pl.when(step < tiles)
    def _():
        full = t_mm(left_ref[...], right_ref[...]).astype(BF)

        @pl.when(is_z(step))
        def _():
            first, _second = lines("z", step)
            for z in range(nz):
                z_own[first.at, z] = full[z * nx * rows : (z + 1) * nx * rows]
            first.start()

        @pl.when(jnp.logical_not(is_z(step)))
        def _():
            first, _second = lines("x", step)
            for x in range(nx):
                for z in range(nz):
                    at = (z * nx + x) * rows
                    x_own[first.at, x, z * rows : (z + 1) * rows, :] = full[at : at + rows]
            first.start()

    def work(kind, tile, lag):
        n1 = nz if kind == "z" else nx
        n2 = nx if kind == "z" else nz
        first, second = lines(kind, tile)
        number = (lag - LAG) // HOP_LAG
        if 1 <= number <= n1 - 1:
            first.stage(number)
            if number == n1 - 1:
                mine = first.own(first.me)

                def keep(total):
                    mine[...] = total.astype(BF)

                first.finish(keep)
                second.start()
        elif number >= n1:
            second.stage(number - n1 + 1)
            if number == n1 + n2 - 2:
                def put(total):
                    @pl.when(tile < in_tiles)
                    def _():
                        win_ref[...] = total

                    @pl.when(tile >= in_tiles)
                    def _():
                        wout_ref[...] = total

                second.finish(put)
                first.sent()
                second.sent()

    for lag in range(last_lag, LAG, -HOP_LAG):
        tile = step - lag
        live = (tile >= 0) & (tile < tiles)
        for kind in ("z", "x"):
            match = is_z(tile) if kind == "z" else jnp.logical_not(is_z(tile))

            @pl.when(live & match)
            def _(kind=kind, tile=tile, lag=lag):
                work(kind, tile, lag)


def weight_grads(left, right, dp_count):
    tok_rows = left.shape[0]
    width = left.shape[1] // 2
    wide = 4 * width
    cols = width // 4
    in_tiles, tiles = wide // cols, (wide + width) // cols
    out_tiles = tiles - in_tiles
    nx = 1 << ((dp_count.bit_length() - 1) // 2)
    nz = dp_count // nx
    rows = width // dp_count
    px, pz = (nx - 1) / nx, (nz - 1) / nz
    x_share = (pz - px / nz) / (px * (1 - 1 / nz) + pz * (1 - 1 / nx))
    z_tiles = max(1, int(tiles * (1 - x_share) + 0.9))
    x_tiles = tiles - z_tiles
    last_lag = LAG + HOP_LAG * (nx + nz - 2)

    def slots(count):
        return count + 1 if count > 2 else 1

    def buffers(count, n1, n2):
        return [
            pltpu.VMEM((count, n1, n2 * rows, cols), BF),
            pltpu.VMEM((count, slots(n1), n2 * rows, cols), BF),
            pltpu.VMEM((count, slots(n2), rows, cols), BF),
        ]

    def semaphores(count, n1, n2):
        return [
            pltpu.SemaphoreType.DMA((count, size)) for size in (n1, slots(n1), n2, slots(n2))
        ]

    return pl.pallas_call(
        functools.partial(weight_kernel, nx, nz, tiles, in_tiles, z_tiles),
        grid=(tiles + last_lag,),
        in_specs=[
            pl.BlockSpec((tok_rows, width), lambda t: (0, jnp.minimum(t, tiles - 1) // in_tiles)),
            pl.BlockSpec((tok_rows, cols), lambda t: (0, jnp.minimum(t, tiles - 1))),
        ],
        out_specs=[
            pl.BlockSpec((rows, cols), lambda t: (0, jnp.clip(t - last_lag, 0, in_tiles - 1))),
            pl.BlockSpec((rows, cols), lambda t: (0, jnp.clip(t - last_lag - in_tiles, 0, out_tiles - 1))),
        ],
        out_shape=[
            jax.ShapeDtypeStruct((rows, wide), F32),
            jax.ShapeDtypeStruct((rows, width), F32),
        ],
        scratch_shapes=buffers(x_tiles, nx, nz) + buffers(z_tiles, nz, nx)
        + semaphores(x_tiles, nx, nz) + semaphores(z_tiles, nz, nx),
        compiler_params=pltpu.CompilerParams(
            vmem_limit_bytes=VMEM_LIMIT, collective_id=1, has_side_effects=True
        ),
        name="weights",
    )(left, right)


def pick(count, most):
    while count % most:
        most -= 1
    return most


def body(saved_inputs, cotangent, pack_lists, segment_ids, w_in, w_out):
    dp_count = lax.axis_size("dp")
    section_count = lax.axis_size("section")
    tok_rows, width = cotangent.shape
    micro_count, rows = segment_ids.shape
    share = tok_rows // dp_count
    group = rows * (256 // (width // H))
    wide = 4 * width
    picked = cotangent[pack_lists[0]]
    positions = jnp.arange(rows)
    allowed = (segment_ids[:, :, None] == jnp.concatenate([segment_ids] * 2, axis=1)[:, None, :]) & (
        jnp.concatenate([positions] * 2)[None, None, :] <= positions[None, :, None]
    )
    mask = (allowed.astype(F32) / rows).reshape(tok_rows, 2 * rows)
    blocks = jnp.arange(group) // rows
    block_mask = (blocks[:, None] == blocks[None, :]).astype(BF)

    def row_spec(tile, cols):
        return pl.BlockSpec((tile, cols), lambda i: (i, 0))

    def whole_spec(shape):
        return pl.BlockSpec(shape, lambda i: (0, 0), pipeline_mode=pl.Buffered(1))

    def whole_spec3(shape):
        return pl.BlockSpec(shape, lambda i: (0, 0, 0), pipeline_mode=pl.Buffered(1))

    tile = rows * pick(micro_count, F_BATCHES)
    f_steps = tok_rows // tile
    cols = [
        (2 * width, BF), (width, BF), (width, BF), (3 * width, BF),
        (wide, BF), (width, BF), (width, BF), (128, F32), (128, F32),
    ]
    packed, xy, gate, mhat, vqk, slope, att, sfac, rx, rm, win_t, wout_t = pl.pallas_call(
        functools.partial(forward_kernel, rows, dp_count, section_count),
        grid=(tok_rows // tile,),
        in_specs=[
            row_spec(tile, width), whole_spec((width, wide)),
            row_spec(tile, 2 * rows), whole_spec((group, group)),
            whole_spec3((dp_count, share, width)),
            pl.BlockSpec((width, wide // f_steps), lambda i: (0, i)),
            pl.BlockSpec((width // f_steps, width), lambda i: (i, 0)),
        ],
        out_specs=[pl.BlockSpec(memory_space=pl.ANY)]
        + [row_spec(tile, n) for n, _ in cols]
        + [pl.BlockSpec((wide // f_steps, width), lambda i: (i, 0)),
           pl.BlockSpec((width, width // f_steps), lambda i: (0, i))],
        out_shape=[jax.ShapeDtypeStruct((dp_count, share, width), BF)]
        + [jax.ShapeDtypeStruct((tok_rows, n), t) for n, t in cols]
        + [jax.ShapeDtypeStruct((wide, width), BF), jax.ShapeDtypeStruct((width, width), BF)],
        scratch_shapes=[
            pltpu.SemaphoreType.DMA((dp_count - 1,)),
            pltpu.SemaphoreType.DMA((dp_count - 1,)),
            pltpu.SemaphoreType.DMA,
        ],
        compiler_params=pltpu.CompilerParams(
            vmem_limit_bytes=VMEM_LIMIT, collective_id=2, has_side_effects=True
        ),
        cost_estimate=pl.CostEstimate(
            flops=2 * tok_rows * width * wide, bytes_accessed=40 << 20, transcendentals=tok_rows * wide
        ),
        name="forward",
    )(
        saved_inputs[0], w_in[0], mask, block_mask, picked.reshape(dp_count, share, width),
        w_in[0], w_out[0],
    )

    tile = rows * pick(micro_count, B_BATCHES)
    steps = tok_rows // tile
    dx, dgrad = pl.pallas_call(
        functools.partial(backward_kernel, rows, section_count),
        grid=(steps,),
        in_specs=[
            row_spec(tile, width), whole_spec((wide, width)), whole_spec((width, width)),
            whole_spec((group, group)), row_spec(tile, width), row_spec(tile, width),
            row_spec(tile, width), row_spec(tile, 3 * width), row_spec(tile, wide),
            row_spec(tile, width), row_spec(tile, width), row_spec(tile, 128), row_spec(tile, 128),
        ],
        out_specs=[row_spec(tile, width), row_spec(tile, wide + width)],
        out_shape=[
            jax.ShapeDtypeStruct((tok_rows, width), BF),
            jax.ShapeDtypeStruct((tok_rows, wide + width), BF),
        ],
        scratch_shapes=[
            pltpu.VMEM((steps, tile, width), BF),
            pltpu.VMEM((steps, tile, width), BF),
            pltpu.SemaphoreType.DMA((steps,)),
            pltpu.SemaphoreType.DMA((steps,)),
        ],
        compiler_params=pltpu.CompilerParams(
            vmem_limit_bytes=VMEM_LIMIT, collective_id=0, has_side_effects=True
        ),
        name="backward",
    )(packed.reshape(tok_rows, width), win_t, wout_t, block_mask, xy, gate, mhat, vqk, slope, att, sfac, rx, rm)

    grad_w_in, grad_w_out = weight_grads(xy, dgrad, dp_count)
    return (dx[None], grad_w_in[None], grad_w_out[None])


def solution(mesh):
    return jax.shard_map(
        body,
        mesh=mesh,
        in_specs=(
            P("section", "dp", None),
            P("dp", None),
            P("dp", None),
            P("dp", None),
            P("section", None, None),
            P("section", None, None),
        ),
        out_specs=(P("section", "dp", None), P("section", "dp", None), P("section", "dp", None)),
        check_vma=False,
    )
```

```python
import functools

import jax
import jax.numpy as jnp
from jax import lax
from jax.experimental import pallas as pl
from jax.experimental.pallas import tpu as pltpu
from jax.sharding import PartitionSpec as P

H = 16
F_BATCHES = 3
B_BATCHES = 2
LAG = 1
HOP_LAG = 3
BF = jnp.bfloat16
F32 = jnp.float32
VMEM_LIMIT = 60 * 1024 * 1024


def mm(a, b):
    return lax.dot_general(a, b, (((1,), (0,)), ((), ())), preferred_element_type=F32)


def mm_t(a, b):
    return lax.dot_general(a, b, (((1,), (1,)), ((), ())), preferred_element_type=F32)


def t_mm(a, b):
    return lax.dot_general(a, b, (((0,), (0,)), ((), ())), preferred_element_type=F32)


def sigmoid(x):
    return 0.5 * jnp.tanh(0.5 * x) + 0.5


def stacked(part, mask, copies):
    return jnp.concatenate([part] * copies, axis=0) * mask


def fill_blocks(ref, rows):
    place = lax.broadcasted_iota(jnp.int32, (rows, ref.shape[1]), 1)
    for lo in range(0, ref.shape[0], rows):
        ref[lo : lo + rows, :] = jnp.where((place >= lo) & (place < lo + rows), 1.0, 0.0).astype(BF)


def norm_stats(values):
    centered = values - jnp.mean(values, axis=-1, keepdims=True)
    variance = jnp.mean(centered * centered, axis=-1, keepdims=True)
    inv = lax.rsqrt(variance + 1e-05)
    return centered * inv, inv


def forward_kernel(
    rows, dp_count, sections, x_ref, w_ref, seg_ref, list_ref, cot_ref,
    win_part_ref, wout_part_ref,
    packed_ref, xy_ref, gate_ref, mhat_ref, vqk_ref, slope_ref, att_ref, sfac_ref, rx_ref, rm_ref,
    win_t_ref, wout_t_ref, bm_ref, before_ref, loaded, picked, send_sem, recv_sem, own_sem,
):
    step = pl.program_id(0)
    last = sections - 1
    section = lax.axis_index("section")
    me = lax.axis_index("dp")
    share = packed_ref.shape[1]

    def hop(peer):
        return pltpu.make_async_remote_copy(
            src_ref=picked.at[pl.ds(pl.multiple_of(peer * share, 16), share)],
            dst_ref=packed_ref.at[me],
            send_sem=send_sem.at[peer],
            recv_sem=recv_sem.at[me],
            device_id={"dp": peer, "section": last},
            device_id_type=pl.DeviceIdType.MESH,
        )

    def greet(other):
        barrier = pltpu.get_barrier_semaphore()
        for peer in range(dp_count):
            pl.semaphore_signal(
                barrier, inc=1, device_id={"dp": peer, "section": other},
                device_id_type=pl.DeviceIdType.MESH,
            )
        pl.semaphore_wait(barrier, dp_count)

    @pl.when(step == 0)
    def _():
        fill_blocks(bm_ref, rows)
        place = lax.broadcasted_iota(jnp.int32, before_ref.shape, 1)
        below = lax.broadcasted_iota(jnp.int32, before_ref.shape, 0)
        for lo in range(0, before_ref.shape[1], rows):
            here = (place >= lo) & (place - lo <= below) & (place < lo + rows)
            kept = jnp.where(here, 1.0 / rows, 0.0)
            before_ref[...] = kept if lo == 0 else before_ref[...] + kept

        @pl.when(section == last)
        def _():
            greet(0)

        @pl.when(section == 0)
        def _():
            load = pltpu.make_async_copy(cot_ref, loaded, own_sem)
            load.start()
            greet(last)
            load.wait()
            count = picked.shape[0]
            cut = list_ref.shape[1] // 3 if list_ref.shape[1] % 384 == 0 else list_ref.shape[1]
            for lo in range(0, count, cut):
                source = lax.broadcasted_iota(jnp.int32, (count, cut), 0)
                chosen = jnp.where(source == list_ref[:, lo : lo + cut], 1.0, 0.0).astype(BF)
                picked[lo : lo + cut, :] = t_mm(chosen, loaded[...]).astype(BF)

    @pl.when((step == 1) & (section == 0))
    def _():
        for peer in range(dp_count):
            hop(peer).start()

    width = x_ref.shape[1]
    group = bm_ref.shape[0]
    copies = group // rows
    head_dim = width // H
    xn, rx = norm_stats(x_ref[...].astype(F32))
    xy_ref[:, :width] = xn.astype(BF)
    rx_ref[...] = jnp.broadcast_to(rx, rx_ref.shape)
    win_t_ref[...] = win_part_ref[...].T
    wout_t_ref[...] = wout_part_ref[...].T
    for part in range(4):
        cols = slice(part * width, (part + 1) * width)
        pre = mm(xy_ref[:, :width], w_ref[:, cols])
        sig = sigmoid(pre)
        act = pre * sig
        slope_ref[:, cols] = (sig + act * (1.0 - sig)).astype(BF)
        if part == 0:
            gate_ref[...] = act.astype(BF)
        else:
            vqk_ref[:, (part - 1) * width : part * width] = act.astype(BF)
    block_mask = bm_ref[...]
    scale = 1.0 / head_dim ** 0.5
    for micro in range(x_ref.shape[0] // rows):
        r = slice(micro * rows, (micro + 1) * rows)
        ids = seg_ref[pl.ds(step * (x_ref.shape[0] // rows) + micro, 1), :].astype(F32)
        ids = jnp.concatenate([ids] * (128 // rows), axis=1)
        turned = jnp.broadcast_to(ids, (128, 128)).T[:rows]
        own_id = jnp.concatenate([turned] * (group // 128), axis=1)
        key_id = jnp.concatenate([ids] * (group // 128), axis=1)
        allowed = jnp.where(own_id == key_id, before_ref[...], 0.0)
        mixed = []
        for lo in range(0, width, group):
            c = slice(lo, lo + group)
            v = vqk_ref[r, lo : lo + group]
            q = vqk_ref[r, width + lo : width + lo + group]
            k = vqk_ref[r, 2 * width + lo : 2 * width + lo + group]
            scores = mm_t(q, stacked(k, block_mask, copies)) * scale
            sig = sigmoid(scores)
            act = scores * sig
            att = (act * allowed).astype(BF)
            att_ref[r, c] = att
            sfac_ref[r, c] = ((sig + act * (1.0 - sig)) * allowed * scale).astype(BF)
            mixed.append(mm(att, stacked(v, block_mask, copies)))
        mixed = jnp.concatenate(mixed, axis=1)
        mhat, rm = norm_stats(mixed)
        mhat_ref[r, :] = mhat.astype(BF)
        rm_ref[r, :] = jnp.broadcast_to(rm, (rows, rm_ref.shape[1]))
        xy_ref[r, width:] = (mhat * gate_ref[r, :].astype(F32)).astype(BF)

    @pl.when(step == pl.num_programs(0) - 1)
    def _():
        @pl.when(section == 0)
        def _():
            for peer in range(dp_count):
                hop(peer).wait_send()

        @pl.when(section == last)
        def _():
            for peer in range(dp_count):
                pltpu.make_async_remote_copy(
                    src_ref=picked.at[pl.ds(0, share)],
                    dst_ref=packed_ref.at[peer],
                    send_sem=send_sem.at[peer],
                    recv_sem=recv_sem.at[peer],
                    device_id={"dp": peer, "section": 0},
                    device_id_type=pl.DeviceIdType.MESH,
                ).wait_recv()


def backward_kernel(
    rows, sections, g0_ref, win_ref, wout_ref, xn_ref, gate_ref, mhat_ref, vqk_ref,
    slope_ref, att_ref, sfac_ref, rx_ref, rm_ref,
    dx_ref, dpre_ref, bm_ref, arrived, leaving, send_sem, recv_sem,
):
    step = pl.program_id(0)
    steps = pl.num_programs(0)
    section = lax.axis_index("section")
    last = sections - 1
    width = g0_ref.shape[1]
    wide = 4 * width
    group = bm_ref.shape[0]
    copies = group // rows
    before = jnp.maximum(section - 1, 0)
    after = jnp.minimum(section + 1, last)

    def hop(slot):
        return pltpu.make_async_remote_copy(
            src_ref=leaving.at[slot],
            dst_ref=arrived.at[slot],
            send_sem=send_sem.at[slot],
            recv_sem=recv_sem.at[slot],
            device_id={"section": before},
            device_id_type=pl.DeviceIdType.MESH,
        )

    @pl.when(step == 0)
    def _():
        fill_blocks(bm_ref, rows)
        barrier = pltpu.get_barrier_semaphore()

        @pl.when(section > 0)
        def _():
            pl.semaphore_signal(
                barrier, inc=1, device_id={"section": before}, device_id_type=pl.DeviceIdType.MESH
            )

        @pl.when(section < last)
        def _():
            pl.semaphore_signal(
                barrier, inc=1, device_id={"section": after}, device_id_type=pl.DeviceIdType.MESH
            )

        peers = (section > 0).astype(jnp.int32) + (section < last).astype(jnp.int32)
        pl.semaphore_wait(barrier, peers)

    @pl.when(section == last)
    def _():
        dpre_ref[:, wide:] = g0_ref[...]

    @pl.when(section < last)
    def _():
        hop(step).wait_recv()
        dpre_ref[:, wide:] = arrived[step]

    gyu = mm(dpre_ref[:, wide:], wout_ref[...]).astype(BF).astype(F32)
    dpre_ref[:, :width] = (gyu * mhat_ref[...].astype(F32) * slope_ref[:, :width].astype(F32)).astype(BF)
    block_mask = bm_ref[...]
    block_mask_f = block_mask.astype(F32)

    def fold(full):
        full = full * block_mask_f
        total = full[:rows]
        for copy in range(1, copies):
            total = total + full[copy * rows : (copy + 1) * rows]
        return total.astype(BF).astype(F32)

    for micro in range(g0_ref.shape[0] // rows):
        r = slice(micro * rows, (micro + 1) * rows)
        dn = gyu[r, :] * gate_ref[r, :].astype(F32)
        mhat = mhat_ref[r, :].astype(F32)
        mean_d = jnp.mean(dn, axis=-1, keepdims=True)
        mean_p = jnp.mean(dn * mhat, axis=-1, keepdims=True)
        dm = (rm_ref[r, :1] * (dn - mean_d - mhat * mean_p)).astype(BF)
        for lo in range(0, width, group):
            c = slice(lo, lo + group)
            cv = slice(lo, lo + group)
            cq = slice(width + lo, width + lo + group)
            ck = slice(2 * width + lo, 2 * width + lo + group)
            dmg = dm[:, lo : lo + group]
            datt = mm_t(dmg, stacked(vqk_ref[r, cv], block_mask, copies)).astype(BF).astype(F32)
            ds = (datt * sfac_ref[r, c].astype(F32)).astype(BF)
            dv = fold(t_mm(att_ref[r, c], dmg))
            dq = mm(ds, stacked(vqk_ref[r, ck], block_mask, copies)).astype(BF).astype(F32)
            dk = fold(t_mm(ds, vqk_ref[r, cq]))
            for part, value in ((1, dv), (2, dq), (3, dk)):
                cols = slice(part * width + lo, part * width + lo + group)
                dpre_ref[r, cols] = (value * slope_ref[r, cols].astype(F32)).astype(BF)
    dn = mm(dpre_ref[:, :wide], win_ref[...])
    xn = xn_ref[...].astype(F32)
    mean_d = jnp.mean(dn, axis=-1, keepdims=True)
    mean_p = jnp.mean(dn * xn, axis=-1, keepdims=True)
    dx = (dpre_ref[:, wide:].astype(F32) + rx_ref[:, :1] * (dn - mean_d - xn * mean_p)).astype(BF)
    dx_ref[...] = dx

    @pl.when(section > 0)
    def _():
        leaving[step] = dx
        hop(step).start()

    @pl.when((section > 0) & (step == steps - 1))
    def _():
        def finish(slot, carry):
            hop(slot).wait_send()
            return carry

        lax.fori_loop(0, steps, finish, 0)


class Line:
    def __init__(self, count, me, device, at, own, landed, send_sem, recv_sem):
        self.count, self.me, self.device, self.at = count, me, device, at
        self.own, self.landed = own, landed
        self.send_sem, self.recv_sem = send_sem, recv_sem

    def base(self, me):
        return self.count - me if me > 0 else 0

    def copy(self, src, slot, shard, peer):
        return pltpu.make_async_remote_copy(
            src_ref=src,
            dst_ref=self.landed.at[self.at, slot],
            send_sem=self.send_sem.at[self.at, shard],
            recv_sem=self.recv_sem.at[self.at, slot],
            device_id=self.device(peer),
            device_id_type=pl.DeviceIdType.MESH,
        )

    def arrive(self, slot):
        self.copy(self.landed.at[self.at, slot], slot, 0, 0).wait_recv()

    def start(self):
        last = self.count - 1

        @pl.when(self.me == 0)
        def _():
            for shard in range(last, 0, -1):
                self.copy(self.own(shard), shard - 1, shard, 1).start()

        @pl.when(self.me == last)
        def _():
            for shard in range(last):
                self.copy(self.own(shard), self.base(last - 1) + shard, shard, last - 1).start()

    def pass_on(self, slot, shard, to_slot, peer):
        self.arrive(slot)
        ref = self.landed.at[self.at, slot]
        ref[...] = (ref[...].astype(F32) + self.own(shard)[...].astype(F32)).astype(BF)
        self.copy(ref, to_slot, shard, peer).start()

    def stage(self, number):
        up, down = number, self.count - 1 - number

        @pl.when(self.me == up)
        def _():
            for shard in range(self.count - 1, up, -1):
                self.pass_on(shard - up, shard, shard - up - 1, up + 1)
            self.arrive(0)

        @pl.when(self.me == down)
        def _():
            for shard in range(down):
                self.pass_on(self.base(down) + shard, shard, self.base(down - 1) + shard, down - 1)
            self.arrive(self.base(down) + down)

    def finish(self, out):
        inner = (self.me > 0) & (self.me < self.count - 1)
        total = self.own(self.me)[...].astype(F32) + self.landed[self.at, 0].astype(F32)
        if self.count == 2:
            out(total)
        else:
            @pl.when(inner)
            def _():
                out(total + self.landed[self.at, self.count].astype(F32))

            @pl.when(jnp.logical_not(inner))
            def _():
                out(total)

    def sent(self):
        for offset in range(1, self.count):
            shard = (self.me + offset) % self.count
            self.copy(self.own(shard), 0, shard, 0).wait_send()


def weight_kernel(
    nx, nz, tiles, in_tiles, z_tiles, left_ref, right_ref, win_ref, wout_ref,
    x_own, x_first, x_second, z_own, z_first, z_second,
    xs1, xr1, xs2, xr2, zs1, zr1, zs2, zr2,
):
    step = pl.program_id(0)
    me = lax.axis_index("dp")
    my_z = me // nx
    my_x = me % nx
    rows = win_ref.shape[0]
    period = tiles // z_tiles
    last_lag = LAG + HOP_LAG * (nx + nz - 2)

    def device(z, x):
        return {"dp": z * nx + x}

    def on_x(peer):
        return device(my_z, peer)

    def on_z(peer):
        return device(peer, my_x)

    def is_z(tile):
        return (tile % period == 0) & (tile // period < z_tiles)

    def lines(kind, tile):
        if kind == "z":
            at = tile // period
            first = Line(nz, my_z, on_z, at, lambda j: z_own.at[at, j], z_first, zs1, zr1)
            second = Line(
                nx, my_x, on_x, at, lambda j: z_own.at[at, my_z, pl.ds(j * rows, rows)], z_second, zs2, zr2
            )
        else:
            at = tile - jnp.minimum((tile + period - 1) // period, z_tiles)
            first = Line(nx, my_x, on_x, at, lambda j: x_own.at[at, j], x_first, xs1, xr1)
            second = Line(
                nz, my_z, on_z, at, lambda j: x_own.at[at, my_x, pl.ds(j * rows, rows)], x_second, xs2, xr2
            )
        return first, second

    @pl.when(step == 0)
    def _():
        barrier = pltpu.get_barrier_semaphore()
        greeted = 0
        for mine, count, to in ((my_x, nx, on_x), (my_z, nz, on_z)):
            for has, peer in ((mine > 0, mine - 1), (mine < count - 1, mine + 1)):
                @pl.when(has)
                def _(peer=peer, to=to):
                    pl.semaphore_signal(
                        barrier, inc=1, device_id=to(peer), device_id_type=pl.DeviceIdType.MESH
                    )

                greeted = greeted + has.astype(jnp.int32)
        pl.semaphore_wait(barrier, greeted)

    @pl.when(step < tiles)
    def _():
        full = t_mm(left_ref[...], right_ref[...]).astype(BF)

        @pl.when(is_z(step))
        def _():
            first, _second = lines("z", step)
            for z in range(nz):
                z_own[first.at, z] = full[z * nx * rows : (z + 1) * nx * rows]
            first.start()

        @pl.when(jnp.logical_not(is_z(step)))
        def _():
            first, _second = lines("x", step)
            for x in range(nx):
                for z in range(nz):
                    at = (z * nx + x) * rows
                    x_own[first.at, x, z * rows : (z + 1) * rows, :] = full[at : at + rows]
            first.start()

    def work(kind, tile, lag):
        n1 = nz if kind == "z" else nx
        n2 = nx if kind == "z" else nz
        first, second = lines(kind, tile)
        number = (lag - LAG) // HOP_LAG
        if 1 <= number <= n1 - 1:
            first.stage(number)
            if number == n1 - 1:
                mine = first.own(first.me)

                def keep(total):
                    mine[...] = total.astype(BF)

                first.finish(keep)
                second.start()
        elif number >= n1:
            second.stage(number - n1 + 1)
            if number == n1 + n2 - 2:
                def put(total):
                    @pl.when(tile < in_tiles)
                    def _():
                        win_ref[...] = total

                    @pl.when(tile >= in_tiles)
                    def _():
                        wout_ref[...] = total

                second.finish(put)
                first.sent()
                second.sent()

    for lag in range(last_lag, LAG, -HOP_LAG):
        tile = step - lag
        live = (tile >= 0) & (tile < tiles)
        for kind in ("z", "x"):
            match = is_z(tile) if kind == "z" else jnp.logical_not(is_z(tile))

            @pl.when(live & match)
            def _(kind=kind, tile=tile, lag=lag):
                work(kind, tile, lag)


def weight_grads(left, right, dp_count):
    tok_rows = left.shape[0]
    width = left.shape[1] // 2
    wide = 4 * width
    cols = width // 4
    in_tiles, tiles = wide // cols, (wide + width) // cols
    out_tiles = tiles - in_tiles
    nx = 1 << ((dp_count.bit_length() - 1) // 2)
    nz = dp_count // nx
    rows = width // dp_count
    px, pz = (nx - 1) / nx, (nz - 1) / nz
    x_share = (pz - px / nz) / (px * (1 - 1 / nz) + pz * (1 - 1 / nx))
    z_tiles = max(1, int(tiles * (1 - x_share) + 0.9))
    x_tiles = tiles - z_tiles
    last_lag = LAG + HOP_LAG * (nx + nz - 2)

    def slots(count):
        return count + 1 if count > 2 else 1

    def buffers(count, n1, n2):
        return [
            pltpu.VMEM((count, n1, n2 * rows, cols), BF),
            pltpu.VMEM((count, slots(n1), n2 * rows, cols), BF),
            pltpu.VMEM((count, slots(n2), rows, cols), BF),
        ]

    def semaphores(count, n1, n2):
        return [
            pltpu.SemaphoreType.DMA((count, size)) for size in (n1, slots(n1), n2, slots(n2))
        ]

    return pl.pallas_call(
        functools.partial(weight_kernel, nx, nz, tiles, in_tiles, z_tiles),
        grid=(tiles + last_lag,),
        in_specs=[
            pl.BlockSpec((tok_rows, width), lambda t: (0, jnp.minimum(t, tiles - 1) // in_tiles)),
            pl.BlockSpec((tok_rows, cols), lambda t: (0, jnp.minimum(t, tiles - 1))),
        ],
        out_specs=[
            pl.BlockSpec((rows, cols), lambda t: (0, jnp.clip(t - last_lag, 0, in_tiles - 1))),
            pl.BlockSpec((rows, cols), lambda t: (0, jnp.clip(t - last_lag - in_tiles, 0, out_tiles - 1))),
        ],
        out_shape=[
            jax.ShapeDtypeStruct((rows, wide), F32),
            jax.ShapeDtypeStruct((rows, width), F32),
        ],
        scratch_shapes=buffers(x_tiles, nx, nz) + buffers(z_tiles, nz, nx)
        + semaphores(x_tiles, nx, nz) + semaphores(z_tiles, nz, nx),
        compiler_params=pltpu.CompilerParams(
            vmem_limit_bytes=VMEM_LIMIT, collective_id=1, has_side_effects=True
        ),
        name="weights",
    )(left, right)


def pick(count, most):
    while count % most:
        most -= 1
    return most


def body(saved_inputs, cotangent, pack_lists, segment_ids, w_in, w_out):
    dp_count = lax.axis_size("dp")
    section_count = lax.axis_size("section")
    tok_rows, width = cotangent.shape
    micro_count, rows = segment_ids.shape
    share = tok_rows // dp_count
    group = rows * (256 // (width // H))
    wide = 4 * width

    def row_spec(tile, cols):
        return pl.BlockSpec((tile, cols), lambda i: (i, 0))

    def whole_spec(shape):
        return pl.BlockSpec(shape, lambda i: (0, 0), pipeline_mode=pl.Buffered(1))

    tile = rows * pick(micro_count, F_BATCHES)
    f_steps = tok_rows // tile
    cols = [
        (2 * width, BF), (width, BF), (width, BF), (3 * width, BF),
        (wide, BF), (width, BF), (width, BF), (128, F32), (128, F32),
    ]
    packed, xy, gate, mhat, vqk, slope, att, sfac, rx, rm, win_t, wout_t = pl.pallas_call(
        functools.partial(forward_kernel, rows, dp_count, section_count),
        grid=(tok_rows // tile,),
        in_specs=[
            row_spec(tile, width), whole_spec((width, wide)),
            whole_spec((micro_count, rows)), whole_spec((1, tok_rows)),
            pl.BlockSpec(memory_space=pl.ANY),
            pl.BlockSpec((width, wide // f_steps), lambda i: (0, i)),
            pl.BlockSpec((width // f_steps, width), lambda i: (i, 0)),
        ],
        out_specs=[pl.BlockSpec(memory_space=pl.ANY)]
        + [row_spec(tile, n) for n, _ in cols]
        + [pl.BlockSpec((wide // f_steps, width), lambda i: (i, 0)),
           pl.BlockSpec((width, width // f_steps), lambda i: (0, i))],
        out_shape=[jax.ShapeDtypeStruct((dp_count, share, width), BF)]
        + [jax.ShapeDtypeStruct((tok_rows, n), t) for n, t in cols]
        + [jax.ShapeDtypeStruct((wide, width), BF), jax.ShapeDtypeStruct((width, width), BF)],
        scratch_shapes=[
            pltpu.VMEM((group, group), BF),
            pltpu.VMEM((rows, group), F32),
            pltpu.VMEM((tok_rows, width), BF),
            pltpu.VMEM((tok_rows, width), BF),
            pltpu.SemaphoreType.DMA((dp_count,)),
            pltpu.SemaphoreType.DMA((dp_count,)),
            pltpu.SemaphoreType.DMA,
        ],
        compiler_params=pltpu.CompilerParams(
            vmem_limit_bytes=VMEM_LIMIT, collective_id=2, has_side_effects=True
        ),
        cost_estimate=pl.CostEstimate(
            flops=2 * tok_rows * width * wide, bytes_accessed=40 << 20, transcendentals=tok_rows * wide
        ),
        name="forward",
    )(
        saved_inputs[0], w_in[0], segment_ids, pack_lists, cotangent,
        w_in[0], w_out[0],
    )

    tile = rows * pick(micro_count, B_BATCHES)
    steps = tok_rows // tile
    dx, dgrad = pl.pallas_call(
        functools.partial(backward_kernel, rows, section_count),
        grid=(steps,),
        in_specs=[
            row_spec(tile, width), whole_spec((wide, width)), whole_spec((width, width)),
            row_spec(tile, width), row_spec(tile, width),
            row_spec(tile, width), row_spec(tile, 3 * width), row_spec(tile, wide),
            row_spec(tile, width), row_spec(tile, width), row_spec(tile, 128), row_spec(tile, 128),
        ],
        out_specs=[row_spec(tile, width), row_spec(tile, wide + width)],
        out_shape=[
            jax.ShapeDtypeStruct((tok_rows, width), BF),
            jax.ShapeDtypeStruct((tok_rows, wide + width), BF),
        ],
        scratch_shapes=[
            pltpu.VMEM((group, group), BF),
            pltpu.VMEM((steps, tile, width), BF),
            pltpu.VMEM((steps, tile, width), BF),
            pltpu.SemaphoreType.DMA((steps,)),
            pltpu.SemaphoreType.DMA((steps,)),
        ],
        compiler_params=pltpu.CompilerParams(
            vmem_limit_bytes=VMEM_LIMIT, collective_id=0, has_side_effects=True
        ),
        name="backward",
    )(packed.reshape(tok_rows, width), win_t, wout_t, xy, gate, mhat, vqk, slope, att, sfac, rx, rm)

    grad_w_in, grad_w_out = weight_grads(xy, dgrad, dp_count)
    return (dx[None], grad_w_in[None], grad_w_out[None])


def solution(mesh):
    return jax.shard_map(
        body,
        mesh=mesh,
        in_specs=(
            P("section", "dp", None),
            P("dp", None),
            P("dp", None),
            P("dp", None),
            P("section", None, None),
            P("section", None, None),
        ),
        out_specs=(P("section", "dp", None), P("section", "dp", None), P("section", "dp", None)),
        check_vma=False,
    )
```

```python
import functools

import jax
import jax.numpy as jnp
from jax import lax
from jax.experimental import pallas as pl
from jax.experimental.pallas import tpu as pltpu
from jax.sharding import PartitionSpec as P

H = 16
F_BATCHES = 3
B_BATCHES = 2
LAG = 1
HOP_LAG = 3
BF = jnp.bfloat16
F32 = jnp.float32
VMEM_LIMIT = 60 * 1024 * 1024


def mm(a, b):
    return lax.dot_general(a, b, (((1,), (0,)), ((), ())), preferred_element_type=F32)


def mm_t(a, b):
    return lax.dot_general(a, b, (((1,), (1,)), ((), ())), preferred_element_type=F32)


def t_mm(a, b):
    return lax.dot_general(a, b, (((0,), (0,)), ((), ())), preferred_element_type=F32)


def sigmoid(x):
    return 0.5 * jnp.tanh(0.5 * x) + 0.5


def stacked(part, mask, copies):
    return jnp.concatenate([part] * copies, axis=0) * mask


def fill_blocks(ref, rows):
    place = lax.broadcasted_iota(jnp.int32, (rows, ref.shape[1]), 1)
    for lo in range(0, ref.shape[0], rows):
        ref[lo : lo + rows, :] = jnp.where((place >= lo) & (place < lo + rows), 1.0, 0.0).astype(BF)


def norm_stats(values):
    centered = values - jnp.mean(values, axis=-1, keepdims=True)
    variance = jnp.mean(centered * centered, axis=-1, keepdims=True)
    inv = lax.rsqrt(variance + 1e-05)
    return centered * inv, inv


def forward_kernel(
    rows, dp_count, sections, x_ref, w_ref, seg_ref, list_ref, cot_ref,
    win_part_ref, wout_part_ref,
    packed_ref, xy_ref, gate_ref, mhat_ref, vqk_ref, slope_ref, att_ref, sfac_ref, rx_ref, rm_ref,
    win_t_ref, wout_t_ref, bm_ref, before_ref, loaded, picked, send_sem, recv_sem, own_sem,
):
    step = pl.program_id(0)
    last = sections - 1
    picker = sections - 2
    section = lax.axis_index("section")
    me = lax.axis_index("dp")
    share = packed_ref.shape[1]

    def hop(peer):
        return pltpu.make_async_remote_copy(
            src_ref=picked.at[pl.ds(pl.multiple_of(peer * share, 16), share)],
            dst_ref=packed_ref.at[me],
            send_sem=send_sem.at[peer],
            recv_sem=recv_sem.at[me],
            device_id={"dp": peer, "section": last},
            device_id_type=pl.DeviceIdType.MESH,
        )

    def greet(other):
        barrier = pltpu.get_barrier_semaphore()
        for peer in range(dp_count):
            pl.semaphore_signal(
                barrier, inc=1, device_id={"dp": peer, "section": other},
                device_id_type=pl.DeviceIdType.MESH,
            )
        pl.semaphore_wait(barrier, dp_count)

    @pl.when(step == 0)
    def _():
        fill_blocks(bm_ref, rows)
        place = lax.broadcasted_iota(jnp.int32, before_ref.shape, 1)
        below = lax.broadcasted_iota(jnp.int32, before_ref.shape, 0)
        for lo in range(0, before_ref.shape[1], rows):
            here = (place >= lo) & (place - lo <= below) & (place < lo + rows)
            kept = jnp.where(here, 1.0 / rows, 0.0)
            before_ref[...] = kept if lo == 0 else before_ref[...] + kept

        @pl.when(section == last)
        def _():
            greet(picker)

        @pl.when(section == picker)
        def _():
            load = pltpu.make_async_copy(cot_ref, loaded, own_sem)
            load.start()
            greet(last)
            load.wait()
            count = picked.shape[0]
            cut = list_ref.shape[1] // 3 if list_ref.shape[1] % 384 == 0 else list_ref.shape[1]
            for lo in range(0, count, cut):
                source = lax.broadcasted_iota(jnp.int32, (count, cut), 0)
                chosen = jnp.where(source == list_ref[:, lo : lo + cut], 1.0, 0.0).astype(BF)
                picked[lo : lo + cut, :] = t_mm(chosen, loaded[...]).astype(BF)
            for offset in range(dp_count):
                hop((me + offset) % dp_count).start()

    width = x_ref.shape[1]
    group = bm_ref.shape[0]
    copies = group // rows
    head_dim = width // H
    xn, rx = norm_stats(x_ref[...].astype(F32))
    xy_ref[:, :width] = xn.astype(BF)
    rx_ref[...] = jnp.broadcast_to(rx, rx_ref.shape)
    win_t_ref[...] = win_part_ref[...].T
    wout_t_ref[...] = wout_part_ref[...].T
    for part in range(4):
        cols = slice(part * width, (part + 1) * width)
        pre = mm(xy_ref[:, :width], w_ref[:, cols])
        sig = sigmoid(pre)
        act = pre * sig
        slope_ref[:, cols] = (sig + act * (1.0 - sig)).astype(BF)
        if part == 0:
            gate_ref[...] = act.astype(BF)
        else:
            vqk_ref[:, (part - 1) * width : part * width] = act.astype(BF)
    block_mask = bm_ref[...]
    scale = 1.0 / head_dim ** 0.5
    for micro in range(x_ref.shape[0] // rows):
        r = slice(micro * rows, (micro + 1) * rows)
        ids = seg_ref[pl.ds(step * (x_ref.shape[0] // rows) + micro, 1), :].astype(F32)
        ids = jnp.concatenate([ids] * (128 // rows), axis=1)
        turned = jnp.broadcast_to(ids, (128, 128)).T[:rows]
        own_id = jnp.concatenate([turned] * (group // 128), axis=1)
        key_id = jnp.concatenate([ids] * (group // 128), axis=1)
        allowed = jnp.where(own_id == key_id, before_ref[...], 0.0)
        mixed = []
        for lo in range(0, width, group):
            c = slice(lo, lo + group)
            v = vqk_ref[r, lo : lo + group]
            q = vqk_ref[r, width + lo : width + lo + group]
            k = vqk_ref[r, 2 * width + lo : 2 * width + lo + group]
            scores = mm_t(q, stacked(k, block_mask, copies)) * scale
            sig = sigmoid(scores)
            act = scores * sig
            att = (act * allowed).astype(BF)
            att_ref[r, c] = att
            sfac_ref[r, c] = ((sig + act * (1.0 - sig)) * allowed * scale).astype(BF)
            mixed.append(mm(att, stacked(v, block_mask, copies)))
        mixed = jnp.concatenate(mixed, axis=1)
        mhat, rm = norm_stats(mixed)
        mhat_ref[r, :] = mhat.astype(BF)
        rm_ref[r, :] = jnp.broadcast_to(rm, (rows, rm_ref.shape[1]))
        xy_ref[r, width:] = (mhat * gate_ref[r, :].astype(F32)).astype(BF)

    @pl.when(step == pl.num_programs(0) - 1)
    def _():
        @pl.when(section == picker)
        def _():
            for peer in range(dp_count):
                hop(peer).wait_send()

        @pl.when(section == last)
        def _():
            for peer in range(dp_count):
                pltpu.make_async_remote_copy(
                    src_ref=picked.at[pl.ds(0, share)],
                    dst_ref=packed_ref.at[peer],
                    send_sem=send_sem.at[peer],
                    recv_sem=recv_sem.at[peer],
                    device_id={"dp": peer, "section": picker},
                    device_id_type=pl.DeviceIdType.MESH,
                ).wait_recv()


def backward_kernel(
    rows, sections, g0_ref, win_ref, wout_ref, xn_ref, gate_ref, mhat_ref, vqk_ref,
    slope_ref, att_ref, sfac_ref, rx_ref, rm_ref,
    dx_ref, dpre_ref, bm_ref, arrived, leaving, send_sem, recv_sem,
):
    step = pl.program_id(0)
    steps = pl.num_programs(0)
    section = lax.axis_index("section")
    last = sections - 1
    width = g0_ref.shape[1]
    wide = 4 * width
    group = bm_ref.shape[0]
    copies = group // rows
    before = jnp.maximum(section - 1, 0)
    after = jnp.minimum(section + 1, last)

    def hop(slot):
        return pltpu.make_async_remote_copy(
            src_ref=leaving.at[slot],
            dst_ref=arrived.at[slot],
            send_sem=send_sem.at[slot],
            recv_sem=recv_sem.at[slot],
            device_id={"section": before},
            device_id_type=pl.DeviceIdType.MESH,
        )

    @pl.when(step == 0)
    def _():
        fill_blocks(bm_ref, rows)
        barrier = pltpu.get_barrier_semaphore()

        @pl.when(section > 0)
        def _():
            pl.semaphore_signal(
                barrier, inc=1, device_id={"section": before}, device_id_type=pl.DeviceIdType.MESH
            )

        @pl.when(section < last)
        def _():
            pl.semaphore_signal(
                barrier, inc=1, device_id={"section": after}, device_id_type=pl.DeviceIdType.MESH
            )

        peers = (section > 0).astype(jnp.int32) + (section < last).astype(jnp.int32)
        pl.semaphore_wait(barrier, peers)

    @pl.when(section == last)
    def _():
        dpre_ref[:, wide:] = g0_ref[...]

    @pl.when(section < last)
    def _():
        hop(step).wait_recv()
        dpre_ref[:, wide:] = arrived[step]

    gyu = mm(dpre_ref[:, wide:], wout_ref[...]).astype(BF).astype(F32)
    dpre_ref[:, :width] = (gyu * mhat_ref[...].astype(F32) * slope_ref[:, :width].astype(F32)).astype(BF)
    block_mask = bm_ref[...]
    block_mask_f = block_mask.astype(F32)

    def fold(full):
        full = full * block_mask_f
        total = full[:rows]
        for copy in range(1, copies):
            total = total + full[copy * rows : (copy + 1) * rows]
        return total.astype(BF).astype(F32)

    for micro in range(g0_ref.shape[0] // rows):
        r = slice(micro * rows, (micro + 1) * rows)
        dn = gyu[r, :] * gate_ref[r, :].astype(F32)
        mhat = mhat_ref[r, :].astype(F32)
        mean_d = jnp.mean(dn, axis=-1, keepdims=True)
        mean_p = jnp.mean(dn * mhat, axis=-1, keepdims=True)
        dm = (rm_ref[r, :1] * (dn - mean_d - mhat * mean_p)).astype(BF)
        for lo in range(0, width, group):
            c = slice(lo, lo + group)
            cv = slice(lo, lo + group)
            cq = slice(width + lo, width + lo + group)
            ck = slice(2 * width + lo, 2 * width + lo + group)
            dmg = dm[:, lo : lo + group]
            datt = mm_t(dmg, stacked(vqk_ref[r, cv], block_mask, copies)).astype(BF).astype(F32)
            ds = (datt * sfac_ref[r, c].astype(F32)).astype(BF)
            dv = fold(t_mm(att_ref[r, c], dmg))
            dq = mm(ds, stacked(vqk_ref[r, ck], block_mask, copies)).astype(BF).astype(F32)
            dk = fold(t_mm(ds, vqk_ref[r, cq]))
            for part, value in ((1, dv), (2, dq), (3, dk)):
                cols = slice(part * width + lo, part * width + lo + group)
                dpre_ref[r, cols] = (value * slope_ref[r, cols].astype(F32)).astype(BF)
    dn = mm(dpre_ref[:, :wide], win_ref[...])
    xn = xn_ref[...].astype(F32)
    mean_d = jnp.mean(dn, axis=-1, keepdims=True)
    mean_p = jnp.mean(dn * xn, axis=-1, keepdims=True)
    dx = (dpre_ref[:, wide:].astype(F32) + rx_ref[:, :1] * (dn - mean_d - xn * mean_p)).astype(BF)
    dx_ref[...] = dx

    @pl.when(section > 0)
    def _():
        leaving[step] = dx
        hop(step).start()

    @pl.when((section > 0) & (step == steps - 1))
    def _():
        def finish(slot, carry):
            hop(slot).wait_send()
            return carry

        lax.fori_loop(0, steps, finish, 0)


class Line:
    def __init__(self, count, me, device, at, own, landed, send_sem, recv_sem):
        self.count, self.me, self.device, self.at = count, me, device, at
        self.own, self.landed = own, landed
        self.send_sem, self.recv_sem = send_sem, recv_sem

    def base(self, me):
        return self.count - me if me > 0 else 0

    def copy(self, src, slot, shard, peer):
        return pltpu.make_async_remote_copy(
            src_ref=src,
            dst_ref=self.landed.at[self.at, slot],
            send_sem=self.send_sem.at[self.at, shard],
            recv_sem=self.recv_sem.at[self.at, slot],
            device_id=self.device(peer),
            device_id_type=pl.DeviceIdType.MESH,
        )

    def arrive(self, slot):
        self.copy(self.landed.at[self.at, slot], slot, 0, 0).wait_recv()

    def start(self):
        last = self.count - 1

        @pl.when(self.me == 0)
        def _():
            for shard in range(last, 0, -1):
                self.copy(self.own(shard), shard - 1, shard, 1).start()

        @pl.when(self.me == last)
        def _():
            for shard in range(last):
                self.copy(self.own(shard), self.base(last - 1) + shard, shard, last - 1).start()

    def pass_on(self, slot, shard, to_slot, peer):
        self.arrive(slot)
        ref = self.landed.at[self.at, slot]
        ref[...] = (ref[...].astype(F32) + self.own(shard)[...].astype(F32)).astype(BF)
        self.copy(ref, to_slot, shard, peer).start()

    def stage(self, number):
        up, down = number, self.count - 1 - number

        @pl.when(self.me == up)
        def _():
            for shard in range(self.count - 1, up, -1):
                self.pass_on(shard - up, shard, shard - up - 1, up + 1)
            self.arrive(0)

        @pl.when(self.me == down)
        def _():
            for shard in range(down):
                self.pass_on(self.base(down) + shard, shard, self.base(down - 1) + shard, down - 1)
            self.arrive(self.base(down) + down)

    def finish(self, out):
        inner = (self.me > 0) & (self.me < self.count - 1)
        total = self.own(self.me)[...].astype(F32) + self.landed[self.at, 0].astype(F32)
        if self.count == 2:
            out(total)
        else:
            @pl.when(inner)
            def _():
                out(total + self.landed[self.at, self.count].astype(F32))

            @pl.when(jnp.logical_not(inner))
            def _():
                out(total)

    def sent(self):
        for offset in range(1, self.count):
            shard = (self.me + offset) % self.count
            self.copy(self.own(shard), 0, shard, 0).wait_send()


def weight_kernel(
    nx, nz, tiles, in_tiles, z_tiles, left_ref, right_ref, win_ref, wout_ref,
    x_own, x_first, x_second, z_own, z_first, z_second,
    xs1, xr1, xs2, xr2, zs1, zr1, zs2, zr2,
):
    step = pl.program_id(0)
    me = lax.axis_index("dp")
    my_z = me // nx
    my_x = me % nx
    rows = win_ref.shape[0]
    period = tiles // z_tiles
    last_lag = LAG + HOP_LAG * (nx + nz - 2)

    def device(z, x):
        return {"dp": z * nx + x}

    def on_x(peer):
        return device(my_z, peer)

    def on_z(peer):
        return device(peer, my_x)

    def is_z(tile):
        return (tile % period == 0) & (tile // period < z_tiles)

    def lines(kind, tile):
        if kind == "z":
            at = tile // period
            first = Line(nz, my_z, on_z, at, lambda j: z_own.at[at, j], z_first, zs1, zr1)
            second = Line(
                nx, my_x, on_x, at, lambda j: z_own.at[at, my_z, pl.ds(j * rows, rows)], z_second, zs2, zr2
            )
        else:
            at = tile - jnp.minimum((tile + period - 1) // period, z_tiles)
            first = Line(nx, my_x, on_x, at, lambda j: x_own.at[at, j], x_first, xs1, xr1)
            second = Line(
                nz, my_z, on_z, at, lambda j: x_own.at[at, my_x, pl.ds(j * rows, rows)], x_second, xs2, xr2
            )
        return first, second

    @pl.when(step == 0)
    def _():
        barrier = pltpu.get_barrier_semaphore()
        greeted = 0
        for mine, count, to in ((my_x, nx, on_x), (my_z, nz, on_z)):
            for has, peer in ((mine > 0, mine - 1), (mine < count - 1, mine + 1)):
                @pl.when(has)
                def _(peer=peer, to=to):
                    pl.semaphore_signal(
                        barrier, inc=1, device_id=to(peer), device_id_type=pl.DeviceIdType.MESH
                    )

                greeted = greeted + has.astype(jnp.int32)
        pl.semaphore_wait(barrier, greeted)

    @pl.when(step < tiles)
    def _():
        full = t_mm(left_ref[...], right_ref[...]).astype(BF)

        @pl.when(is_z(step))
        def _():
            first, _second = lines("z", step)
            for z in range(nz):
                z_own[first.at, z] = full[z * nx * rows : (z + 1) * nx * rows]
            first.start()

        @pl.when(jnp.logical_not(is_z(step)))
        def _():
            first, _second = lines("x", step)
            for x in range(nx):
                for z in range(nz):
                    at = (z * nx + x) * rows
                    x_own[first.at, x, z * rows : (z + 1) * rows, :] = full[at : at + rows]
            first.start()

    def work(kind, tile, lag):
        n1 = nz if kind == "z" else nx
        n2 = nx if kind == "z" else nz
        first, second = lines(kind, tile)
        number = (lag - LAG) // HOP_LAG
        if 1 <= number <= n1 - 1:
            first.stage(number)
            if number == n1 - 1:
                mine = first.own(first.me)

                def keep(total):
                    mine[...] = total.astype(BF)

                first.finish(keep)
                second.start()
        elif number >= n1:
            second.stage(number - n1 + 1)
            if number == n1 + n2 - 2:
                def put(total):
                    @pl.when(tile < in_tiles)
                    def _():
                        win_ref[...] = total

                    @pl.when(tile >= in_tiles)
                    def _():
                        wout_ref[...] = total

                second.finish(put)
                first.sent()
                second.sent()

    for lag in range(last_lag, LAG, -HOP_LAG):
        tile = step - lag
        live = (tile >= 0) & (tile < tiles)
        for kind in ("z", "x"):
            match = is_z(tile) if kind == "z" else jnp.logical_not(is_z(tile))

            @pl.when(live & match)
            def _(kind=kind, tile=tile, lag=lag):
                work(kind, tile, lag)


def weight_grads(left, right, dp_count):
    tok_rows = left.shape[0]
    width = left.shape[1] // 2
    wide = 4 * width
    cols = width // 4
    in_tiles, tiles = wide // cols, (wide + width) // cols
    out_tiles = tiles - in_tiles
    nx = 1 << ((dp_count.bit_length() - 1) // 2)
    nz = dp_count // nx
    rows = width // dp_count
    px, pz = (nx - 1) / nx, (nz - 1) / nz
    x_share = (pz - px / nz) / (px * (1 - 1 / nz) + pz * (1 - 1 / nx))
    z_tiles = max(1, int(tiles * (1 - x_share) + 0.9))
    x_tiles = tiles - z_tiles
    last_lag = LAG + HOP_LAG * (nx + nz - 2)

    def slots(count):
        return count + 1 if count > 2 else 1

    def buffers(count, n1, n2):
        return [
            pltpu.VMEM((count, n1, n2 * rows, cols), BF),
            pltpu.VMEM((count, slots(n1), n2 * rows, cols), BF),
            pltpu.VMEM((count, slots(n2), rows, cols), BF),
        ]

    def semaphores(count, n1, n2):
        return [
            pltpu.SemaphoreType.DMA((count, size)) for size in (n1, slots(n1), n2, slots(n2))
        ]

    return pl.pallas_call(
        functools.partial(weight_kernel, nx, nz, tiles, in_tiles, z_tiles),
        grid=(tiles + last_lag,),
        in_specs=[
            pl.BlockSpec((tok_rows, width), lambda t: (0, jnp.minimum(t, tiles - 1) // in_tiles)),
            pl.BlockSpec((tok_rows, cols), lambda t: (0, jnp.minimum(t, tiles - 1))),
        ],
        out_specs=[
            pl.BlockSpec((rows, cols), lambda t: (0, jnp.clip(t - last_lag, 0, in_tiles - 1))),
            pl.BlockSpec((rows, cols), lambda t: (0, jnp.clip(t - last_lag - in_tiles, 0, out_tiles - 1))),
        ],
        out_shape=[
            jax.ShapeDtypeStruct((rows, wide), F32),
            jax.ShapeDtypeStruct((rows, width), F32),
        ],
        scratch_shapes=buffers(x_tiles, nx, nz) + buffers(z_tiles, nz, nx)
        + semaphores(x_tiles, nx, nz) + semaphores(z_tiles, nz, nx),
        compiler_params=pltpu.CompilerParams(
            vmem_limit_bytes=VMEM_LIMIT, collective_id=1, has_side_effects=True
        ),
        name="weights",
    )(left, right)


def pick(count, most):
    while count % most:
        most -= 1
    return most


def body(saved_inputs, cotangent, pack_lists, segment_ids, w_in, w_out):
    dp_count = lax.axis_size("dp")
    section_count = lax.axis_size("section")
    tok_rows, width = cotangent.shape
    micro_count, rows = segment_ids.shape
    share = tok_rows // dp_count
    group = rows * (256 // (width // H))
    wide = 4 * width

    def row_spec(tile, cols):
        return pl.BlockSpec((tile, cols), lambda i: (i, 0))

    def whole_spec(shape):
        return pl.BlockSpec(shape, lambda i: (0, 0), pipeline_mode=pl.Buffered(1))

    tile = rows * pick(micro_count, F_BATCHES)
    f_steps = tok_rows // tile
    cols = [
        (2 * width, BF), (width, BF), (width, BF), (3 * width, BF),
        (wide, BF), (width, BF), (width, BF), (128, F32), (128, F32),
    ]
    packed, xy, gate, mhat, vqk, slope, att, sfac, rx, rm, win_t, wout_t = pl.pallas_call(
        functools.partial(forward_kernel, rows, dp_count, section_count),
        grid=(tok_rows // tile,),
        in_specs=[
            row_spec(tile, width), whole_spec((width, wide)),
            whole_spec((micro_count, rows)), whole_spec((1, tok_rows)),
            pl.BlockSpec(memory_space=pl.ANY),
            pl.BlockSpec((width, wide // f_steps), lambda i: (0, i)),
            pl.BlockSpec((width // f_steps, width), lambda i: (i, 0)),
        ],
        out_specs=[pl.BlockSpec(memory_space=pl.ANY)]
        + [row_spec(tile, n) for n, _ in cols]
        + [pl.BlockSpec((wide // f_steps, width), lambda i: (i, 0)),
           pl.BlockSpec((width, width // f_steps), lambda i: (0, i))],
        out_shape=[jax.ShapeDtypeStruct((dp_count, share, width), BF)]
        + [jax.ShapeDtypeStruct((tok_rows, n), t) for n, t in cols]
        + [jax.ShapeDtypeStruct((wide, width), BF), jax.ShapeDtypeStruct((width, width), BF)],
        scratch_shapes=[
            pltpu.VMEM((group, group), BF),
            pltpu.VMEM((rows, group), F32),
            pltpu.VMEM((tok_rows, width), BF),
            pltpu.VMEM((tok_rows, width), BF),
            pltpu.SemaphoreType.DMA((dp_count,)),
            pltpu.SemaphoreType.DMA((dp_count,)),
            pltpu.SemaphoreType.DMA,
        ],
        compiler_params=pltpu.CompilerParams(
            vmem_limit_bytes=VMEM_LIMIT, collective_id=2, has_side_effects=True
        ),
        cost_estimate=pl.CostEstimate(
            flops=2 * tok_rows * width * wide, bytes_accessed=40 << 20, transcendentals=tok_rows * wide
        ),
        name="forward",
    )(
        saved_inputs[0], w_in[0], segment_ids, pack_lists, cotangent,
        w_in[0], w_out[0],
    )

    tile = rows * pick(micro_count, B_BATCHES)
    steps = tok_rows // tile
    dx, dgrad = pl.pallas_call(
        functools.partial(backward_kernel, rows, section_count),
        grid=(steps,),
        in_specs=[
            row_spec(tile, width), whole_spec((wide, width)), whole_spec((width, width)),
            row_spec(tile, width), row_spec(tile, width),
            row_spec(tile, width), row_spec(tile, 3 * width), row_spec(tile, wide),
            row_spec(tile, width), row_spec(tile, width), row_spec(tile, 128), row_spec(tile, 128),
        ],
        out_specs=[row_spec(tile, width), row_spec(tile, wide + width)],
        out_shape=[
            jax.ShapeDtypeStruct((tok_rows, width), BF),
            jax.ShapeDtypeStruct((tok_rows, wide + width), BF),
        ],
        scratch_shapes=[
            pltpu.VMEM((group, group), BF),
            pltpu.VMEM((steps, tile, width), BF),
            pltpu.VMEM((steps, tile, width), BF),
            pltpu.SemaphoreType.DMA((steps,)),
            pltpu.SemaphoreType.DMA((steps,)),
        ],
        compiler_params=pltpu.CompilerParams(
            vmem_limit_bytes=VMEM_LIMIT, collective_id=0, has_side_effects=True
        ),
        name="backward",
    )(packed.reshape(tok_rows, width), win_t, wout_t, xy, gate, mhat, vqk, slope, att, sfac, rx, rm)

    grad_w_in, grad_w_out = weight_grads(xy, dgrad, dp_count)
    return (dx[None], grad_w_in[None], grad_w_out[None])


def solution(mesh):
    return jax.shard_map(
        body,
        mesh=mesh,
        in_specs=(
            P("section", "dp", None),
            P("dp", None),
            P("dp", None),
            P("dp", None),
            P("section", None, None),
            P("section", None, None),
        ),
        out_specs=(P("section", "dp", None), P("section", "dp", None), P("section", "dp", None)),
        check_vma=False,
    )
```
